32 devices in a mesh: dp: 8 (over z, core), tensor: 4 (over y, x).
Axes of the slice: x: 2, y: 2, z: 4, core: 2. Of those that a mesh axis runs over, the one named last changes fastest.
Arguments:
- tokens: bfloat16 [4096, 2304], P(('dp', 'tensor')), may hold values from -6 to 6
- cotangent: bfloat16 [4096, 2304], P(('dp', 'tensor')), may hold values from -6 to 6
- doc_lengths: int32 [8, 4], P('dp'), may hold values from 0 to 512, as said below
- w_query: bfloat16 [2304, 2048], P('dp', 'tensor')
- w_key: bfloat16 [2304, 1024], P('dp')
- w_value: bfloat16 [2304, 1024], P('dp'), may hold values from -0.125 to 0.125
- w_out: bfloat16 [2048, 2304], P('tensor', 'dp'), may hold values from -0.125 to 0.125
- w_gate: bfloat16 [2304, 9216], P('dp', 'tensor'), may hold values from -0.125 to 0.125
- w_up: bfloat16 [2304, 9216], P('dp', 'tensor'), may hold values from -0.125 to 0.125
- w_down: bfloat16 [9216, 2304], P('tensor', 'dp'), may hold values from -0.0625 to 0.0625
- norm_gains: bfloat16 [4, 2304], P(None, 'dp'), may hold values from 0.099609375 to 1.8984375
Outputs:
- result: float32 [4096, 2304], P(('dp', 'tensor'))
- grad_tokens: float32 [4096, 2304], P(('dp', 'tensor'))
- grad_query: float32 [2304, 2048], P('dp', 'tensor')
- grad_key: float32 [2304, 1024], P('dp')
- grad_value: float32 [2304, 1024], P('dp')
- grad_out: float32 [2048, 2304], P('tensor', 'dp')
- grad_gate: float32 [2304, 9216], P('dp', 'tensor')
- grad_up: float32 [2304, 9216], P('dp', 'tensor')
- grad_down: float32 [9216, 2304], P('tensor', 'dp')
- grad_gains: float32 [4, 2304], P(None, 'dp')
The draws below stay inside these ranges and needn't reach their ends.
Inputs may be any that keep to these rules, and one draw needn't show every extreme that they name: `doc_lengths`: each row lists the lengths of the documents packed in order from the first token slot of one dp index; a length may be 0; a row sums to between 256 and 512, some row sums to exactly 512, and some document has exactly 512 tokens.
All inputs are finite; a program needn't handle non-finite values.
Results may differ from the reference program's by a relative error of at most 0.015.
The reference program's roundings to bfloat16 on the way count: a program that leaves them out, or rounds other values in their place, can miss the bound.
Values may be sent and summed in bfloat16 or wider, within the bound.
No kernel may reach another device: no remote copies, remote signals or barrier semaphores. Data moves between devices by JAX's collectives and lax.ppermute only.
A program may use at most 192 MiB of HBM per device.

```python
import jax
import jax.numpy as jnp
from jax import lax

D = 2304
HQ = 8
KVH = 4
HD = 256
FF = 9216
DOCS = 4
GROUPS = 8
GROUP_SIZE = 512
MOST = 512
TOKENS = 4096


def draw_doc_lengths(key, part):
    key_total, key_pick, key_sizes = jax.random.split(key, 3)
    totals = jax.random.randint(key_total, (GROUPS,), GROUP_SIZE // 2, GROUP_SIZE + 1)
    fullest = jax.random.randint(key_pick, (), 0, GROUPS)
    least_size = max(1, -(-GROUP_SIZE // DOCS))
    doc_sizes = jax.random.randint(key_sizes, (GROUPS, DOCS), least_size, MOST + 1)
    chosen = jnp.arange(GROUPS) == fullest
    totals = jnp.where(chosen, GROUP_SIZE, totals)
    doc_sizes = doc_sizes.at[:, 0].set(jnp.where(chosen, MOST, doc_sizes[:, 0]))
    before = jnp.cumsum(doc_sizes, axis=1) - doc_sizes
    return jnp.clip(totals[:, None] - before, 0, doc_sizes).astype(jnp.int32)


def head_factors(key, count, top):
    order = jax.random.permutation(key, count).astype(jnp.float32)
    return top ** (order / max(1, count - 1))


def base_entries(key, shape):
    entries = jnp.clip(jax.random.normal(key, shape, jnp.float32), -6.0, 6.0)
    return entries * D ** (-0.5)


def draw_w_query(key, part):
    key_base = jax.random.fold_in(key, 11)
    key_order = jax.random.fold_in(key, 12)
    entries = base_entries(key_base, (D, HQ, HD))
    factors = head_factors(key_order, HQ, 5.0)
    return (entries * factors[None, :, None]).reshape(D, HQ * HD).astype(jnp.bfloat16)


def draw_w_key(key, part):
    key_base = jax.random.fold_in(key, 21)
    key_order = jax.random.fold_in(key, 22)
    entries = base_entries(key_base, (D, KVH, HD))
    factors = head_factors(key_order, KVH, 4.0)
    return (entries * factors[None, :, None]).reshape(D, KVH * HD).astype(jnp.bfloat16)


def raised(values, stream_key, source, target, blocks, factor):
    def block_of(position):
        return (jnp.arange(values.shape[position]) // (values.shape[position] // blocks)).reshape((-1,) + (1,) * (values.ndim - 1 - position))

    one_side = jax.random.permutation(stream_key, blocks)[block_of(target)]
    far = (block_of(target) + blocks // 2) % blocks
    return jnp.where((block_of(source) == one_side) | (block_of(source) == far), factor * values, values)


def level_of(stream_key, dims, pieces, low, largest):
    factor_of, own = 1.0, jax.random.fold_in(stream_key, 6)
    for dim, parts in pieces:
        steps = jnp.exp(jax.random.uniform(jax.random.fold_in(own, dim), (parts,), jnp.float32, low / len(pieces), largest / len(pieces)))
        factor_of = factor_of * jnp.repeat(steps, dims[dim] // parts).reshape([-1 if axis == dim else 1 for axis in range(len(dims))])
    return factor_of


def normal_values(rng, shape, scale, most, pieces=(), kind=jnp.bfloat16):
    values = scale * jax.random.normal(rng, shape, jnp.float32)
    if pieces:
        values = values * level_of(rng, shape, pieces, -0.22, 0.18)
    return jnp.clip(values, -most, most).astype(kind)


def noise_with(own_key, dims, width, most, shards, heavy, kind=jnp.bfloat16):
    values = width * jax.random.normal(own_key, dims, jnp.float32)
    if shards:
        values = values * level_of(own_key, dims, shards, -0.22, 0.18)
    return jnp.clip(raised(values, jax.random.fold_in(own_key, 3), *heavy), -most, most).astype(kind)


def setup_inputs(seed: int = 0) -> dict:
    streams_of = jax.random.split(jax.random.key(seed), 12)
    tokens = normal_values(streams_of[0], (TOKENS, D), 1.0, 6.0, ((0, 32),))
    cotangent = noise_with(streams_of[1], (TOKENS, D), 1.0, 6.0, ((0, 32),), (0, 1, 32, 2.75))
    doc_lengths = draw_doc_lengths(jax.random.fold_in(streams_of[11], 71), 0)
    w_query = draw_w_query(jax.random.fold_in(streams_of[11], 71), 0)
    w_key = draw_w_key(jax.random.fold_in(streams_of[11], 71), 0)
    w_value = normal_values(streams_of[5], (D, KVH * HD), D ** -0.5, 0.125, ((0, 8),))
    w_out = normal_values(streams_of[6], (HQ * HD, D), (HQ * HD) ** -0.5, 0.125, ((0, 4), (1, 8)))
    w_gate = normal_values(streams_of[7], (D, FF), D ** -0.5, 0.125, ((0, 8), (1, 4)))
    w_up = normal_values(streams_of[8], (D, FF), D ** -0.5, 0.125, ((0, 8), (1, 4)))
    w_down = normal_values(streams_of[9], (FF, D), FF ** -0.5, 0.0625, ((0, 4), (1, 8)))
    norm_gains = jnp.clip(1.0 + 0.18 * jax.random.normal(streams_of[10], (4, D), jnp.float32), 0.099609375, 1.8984375).astype(jnp.bfloat16)
    return {"tokens": tokens, "cotangent": cotangent, "doc_lengths": doc_lengths, "w_query": w_query, "w_key": w_key, "w_value": w_value, "w_out": w_out, "w_gate": w_gate, "w_up": w_up, "w_down": w_down, "norm_gains": norm_gains}


EPSILON = 1e-06
SOFT_CAP = 50.0

@jax.custom_vjp
def low(v):
    return lax.optimization_barrier(v.astype(jnp.bfloat16)).astype(jnp.float32)

@jax.custom_vjp
def low_back(v):
    return v

def low_keep(v):
    return (low(v), None)

def low_pass(kept, grad):
    return (grad,)

def back_keep(v):
    return (v, None)

def back_low(kept, grad):
    return (low(grad),)
low.defvjp(low_keep, low_pass)
low_back.defvjp(back_keep, back_low)

def matmul(left, right):
    return jnp.dot(left, right, precision=lax.Precision.HIGHEST, preferred_element_type=jnp.float32)

def rms_norm(source, gain_row):
    return source * lax.rsqrt(lax.optimization_barrier(jnp.mean(source * source, axis=-1, keepdims=True)) + EPSILON) * gain_row

def segment_ids(doc_sizes):
    doc_ends = jnp.cumsum(doc_sizes).astype(jnp.int32)
    places = jnp.arange(GROUP_SIZE, dtype=jnp.int32)
    inside = lax.optimization_barrier(jnp.sum((doc_ends[None, :] <= places[:, None]).astype(jnp.int32), axis=1)).astype(jnp.int32)
    return jnp.where(places >= doc_ends[-1], DOCS + places, inside).astype(jnp.int32)

def one_group(group_tokens, segment, params):
    w_query, w_key, w_value, w_out, w_gate, w_up, w_down, norm_scale = params
    places = jnp.arange(GROUP_SIZE, dtype=jnp.int32)
    normed_attn = low(rms_norm(group_tokens, norm_scale[0]))
    query_all = low(low_back(matmul(normed_attn, w_query))).reshape(GROUP_SIZE, HQ, HD)
    key_heads = low(matmul(normed_attn, w_key)).reshape(GROUP_SIZE, KVH, HD)
    value_heads = low(matmul(normed_attn, w_value)).reshape(GROUP_SIZE, KVH, HD)
    key_copies = low_back(jnp.repeat(key_heads, HQ // KVH, axis=1))
    value_copies = low_back(jnp.repeat(value_heads, HQ // KVH, axis=1))
    raw_scores = low_back(jnp.einsum('qhd,khd->hqk', query_all, key_copies, precision=lax.Precision.HIGHEST))
    capped = SOFT_CAP * jnp.tanh(raw_scores * (HD ** (-0.5) / SOFT_CAP))
    allowed = (segment[:, None] == segment[None, :]) & (places[None, :] <= places[:, None])
    masked = jnp.where(allowed[None], capped, -1e+30)
    row_top = lax.optimization_barrier(jnp.max(masked, axis=-1, keepdims=True))
    shifted = jnp.where(allowed[None], capped - row_top, -200.0)
    exp_scores = jnp.where(allowed[None], jnp.exp(shifted), 0.0)
    prob_rows = low(exp_scores / lax.optimization_barrier(jnp.sum(exp_scores, axis=-1, keepdims=True)))
    attended = low(low_back(jnp.einsum('hqk,khd->qhd', prob_rows, value_copies, precision=lax.Precision.HIGHEST)))
    attended = attended.reshape(GROUP_SIZE, HQ * HD)
    attn_mixed = low_back(matmul(attended, w_out))
    middle = group_tokens + rms_norm(attn_mixed, norm_scale[1])
    normed_ffn = low(rms_norm(middle, norm_scale[2]))
    gate_out = low_back(matmul(normed_ffn, w_gate))
    up_out = low_back(matmul(normed_ffn, w_up))
    hidden = low(jax.nn.gelu(gate_out, approximate=True) * up_out)
    branch = low_back(matmul(hidden, w_down))
    return middle + rms_norm(branch, norm_scale[3])

def reference(tokens, cotangent, doc_lengths, w_query, w_key, w_value, w_out, w_gate, w_up, w_down, norm_gains):
    segments = jax.vmap(segment_ids)(doc_lengths)
    checked = jax.checkpoint(one_group)

    def forward(stream, *params):
        grouped = stream.reshape(GROUPS, GROUP_SIZE, D)
        outputs = lax.map(lambda member: checked(member[0], member[1], params), (grouped, segments))
        return outputs.reshape(TOKENS, D)
    weights = tuple((matrix.astype(jnp.float32) for matrix in (w_query, w_key, w_value, w_out, w_gate, w_up, w_down, norm_gains)))
    result, pullback = jax.vjp(forward, tokens.astype(jnp.float32), *weights)
    gradients = pullback(cotangent.astype(jnp.float32))
    return (result, gradients[0], gradients[1], gradients[2], gradients[3], gradients[4], gradients[5], gradients[6], gradients[7], gradients[8])
```

```python
import jax
import jax.numpy as jnp
from jax import lax
from jax.sharding import PartitionSpec as P

HQ = 8
KVH = 4
HD = 256

EPSILON = 1e-06
SOFT_CAP = 50.0
BF = jnp.bfloat16
F32 = jnp.float32
BOTH = ("dp", "tensor")


def inv_root(source):
    return lax.rsqrt(jnp.mean(source * source, axis=-1, keepdims=True) + EPSILON)


def norm_back(source, inverse, gain_row, upstream):
    unit_rows = source * inverse
    scaled = upstream * gain_row
    grad_input = inverse * (
        scaled - unit_rows * jnp.mean(scaled * unit_rows, axis=-1, keepdims=True)
    )
    return (grad_input, jnp.sum(upstream * unit_rows, axis=0))


def gated_unit(gate_in, up_in):
    return jax.nn.gelu(gate_in, approximate=True) * up_in


def dot_nn(left, right):
    return jnp.dot(left, right, preferred_element_type=F32)


def dot_nt(left, right):
    return lax.dot_general(left, right, (((1,), (1,)), ((), ())), preferred_element_type=F32)


def dot_tn(left, right):
    return lax.dot_general(left, right, (((0,), (0,)), ((), ())), preferred_element_type=F32)


class Grid:
    def __init__(self, dp, tp):
        self.dp, self.tp = dp, tp
        self.nz, self.nc = dp // 2, 2
        self.ny, self.nx = 2, tp // 2

    def coords(self, flat):
        d, t = divmod(flat, self.tp)
        z, c = divmod(d, self.nc)
        y, x = divmod(t, self.nx)
        return z, c, y, x

    def flat(self, z, c, y, x):
        return (z * self.nc + c) * self.tp + y * self.nx + x

    def move(self, value, where):
        pairs = []
        for i in range(self.dp * self.tp):
            pairs.append((i, self.flat(*where(*self.coords(i)))))
        return lax.ppermute(value, BOTH, pairs)

    def rot_z(self, value, k=1):
        return self.move(value, lambda z, c, y, x: ((z + k) % self.nz, c, y, x))

    def swap_c(self, value):
        return self.move(value, lambda z, c, y, x: (z, 1 - c, y, x))

    def swap_y(self, value):
        return self.move(value, lambda z, c, y, x: (z, c, 1 - y, x))

    def xor_x(self, value, k):
        return self.move(value, lambda z, c, y, x: (z, c, y, x ^ k))

    def xor_t(self, value, k):
        def where(z, c, y, x):
            t = (y * self.nx + x) ^ k
            return z, c, t // self.nx, t % self.nx

        return self.move(value, where)

    def xor_dp(self, value, k):
        def where(z, c, y, x):
            d = (z * self.nc + c) ^ k
            return d // self.nc, d % self.nc, y, x

        return self.move(value, where)


def pick(stack, index, axis=0):
    return lax.dynamic_index_in_dim(stack, index, axis, keepdims=False)


def put(buffer, piece, *indices):
    start = tuple(indices) + (0,) * (buffer.ndim - len(indices))
    shaped = piece.reshape((1,) * len(indices) + piece.shape)
    return lax.dynamic_update_slice(buffer, shaped, start)


def program(
    grid,
    tokens,
    cotangent,
    doc_lengths,
    w_query,
    w_key,
    w_value,
    w_out,
    w_gate,
    w_up,
    w_down,
    norm_gains,
):
    nz, tp, nx = grid.nz, grid.tp, grid.nx
    dp_index = lax.axis_index("dp")
    t_index = lax.axis_index("tensor")
    z, c = dp_index // grid.nc, dp_index % grid.nc
    rows, width = tokens.shape
    dpart = w_query.shape[0]
    hidden_part = w_gate.shape[1]
    slot = hidden_part // nz
    group_size = rows * tp
    local_heads = w_query.shape[1] // HD
    local_kv = max(1, local_heads * KVH // HQ)
    copies = local_heads // local_kv
    kv_first = t_index * (local_heads * KVH) // HQ
    q_cols, kv_cols = local_heads * HD, local_kv * HD
    from_z = [(z - k) % nz for k in range(nz)]

    gains_other = grid.swap_c(norm_gains)
    gain_pair = jnp.where(
        c == 0, jnp.stack([norm_gains, gains_other]), jnp.stack([gains_other, norm_gains])
    )
    gain_buffer = jnp.zeros((nz,) + gain_pair.shape, BF)
    for k in range(nz):
        gain_buffer = put(gain_buffer, gain_pair if k == 0 else grid.rot_z(gain_pair, k), from_z[k])
    norm_scale = jnp.transpose(gain_buffer, (2, 0, 1, 3)).reshape(4, width).astype(F32)

    key_part = lax.dynamic_slice_in_dim(w_key, kv_first * HD, kv_cols, 1)
    value_part = lax.dynamic_slice_in_dim(w_value, kv_first * HD, kv_cols, 1)

    def gather_dp(local):
        pieces = [local]
        for k in range(1, nz):
            pieces.append(grid.rot_z(pieces[-1]))
        buffer = jnp.zeros((nz, 2) + local.shape, BF)
        for k in range(nz):
            buffer = put(buffer, pieces[k], from_z[k], c)
            buffer = put(buffer, grid.swap_c(pieces[k]), from_z[k], 1 - c)
        return buffer.reshape(width, local.shape[1]), pieces[-1]

    qkv_weight, last_piece = gather_dp(jnp.concatenate([w_query, key_part, value_part], axis=1))
    out_local, last_piece = lax.optimization_barrier((w_out.T, last_piece))
    out_weight_t, last_piece = gather_dp(out_local)

    def by_slot(matrix):
        return jnp.transpose(matrix.reshape(dpart, nz, slot), (1, 0, 2))

    down_slots = jnp.transpose(w_down.reshape(nz, slot, dpart), (0, 2, 1))
    slots, last_piece = lax.optimization_barrier(
        ((by_slot(w_gate), by_slot(w_up), down_slots), last_piece)
    )

    def spread(stack):
        buffer = jnp.zeros((nz, 2, dpart, nx * slot), BF)
        for k in range(nz):
            mine = pick(stack, (z + k) % nz)
            piece = mine if k == 0 else grid.rot_z(mine, k)
            joined = jnp.concatenate(
                [piece] + [grid.xor_x(piece, j) for j in range(1, nx)], axis=1
            )
            buffer = put(buffer, joined, from_z[k], c)
            buffer = put(buffer, grid.swap_c(joined), from_z[k], 1 - c)
        return buffer.reshape(width, nx * slot)

    gate_weight, up_weight, down_weight_t = (spread(stack) for stack in slots)

    place_parts = [(t_index ^ k) * rows + jnp.arange(rows, dtype=jnp.int32) for k in range(tp)]
    places = jnp.concatenate(place_parts)
    doc_ends = jnp.cumsum(doc_lengths[0])
    inside = jnp.sum((doc_ends[None, :] <= places[:, None]).astype(jnp.int32), axis=1)
    segment = jnp.where(places >= doc_ends[-1], doc_lengths.shape[1] + places, inside)
    block_count = max(1, group_size // 512)
    block_rows = group_size // block_count
    qk_scale = HD ** (-0.5)

    def gather_t(unit):
        return jnp.concatenate([unit] + [grid.xor_t(unit, k) for k in range(1, tp)], axis=0)

    def scatter_t(partial):
        total = partial[:rows]
        for k in range(1, tp):
            total = total + grid.xor_t(partial[k * rows : (k + 1) * rows].astype(BF), k).astype(F32)
        return total

    def block_scores(first_row, query_all, key_copies):
        query_block = query_all[first_row : first_row + block_rows]
        raw_scores = jnp.einsum(
            "qhd,khd->hqk", query_block, key_copies, preferred_element_type=F32
        )
        bent_scores = jnp.tanh(raw_scores * (qk_scale / SOFT_CAP))
        row_segment = segment[first_row : first_row + block_rows]
        row_places = places[first_row : first_row + block_rows]
        allowed = (row_segment[:, None] == segment[None, :]) & (
            places[None, :] <= row_places[:, None]
        )
        return (query_block, bent_scores, allowed)

    stream = tokens.astype(F32)
    scale_in = inv_root(stream)
    normed_attn = (stream * scale_in * norm_scale[0]).astype(BF)
    attn_gathered = gather_t(normed_attn)
    qkv = dot_nn(attn_gathered, qkv_weight).astype(BF)
    query_all = qkv[:, :q_cols].reshape(group_size, local_heads, HD)
    key_heads = qkv[:, q_cols : q_cols + kv_cols].reshape(group_size, local_kv, HD)
    value_heads = qkv[:, q_cols + kv_cols :].reshape(group_size, local_kv, HD)
    key_copies = jnp.repeat(key_heads, copies, axis=1)
    value_copies = jnp.repeat(value_heads, copies, axis=1)
    head_outs = []
    log_totals = []
    for block_number in range(block_count):
        first_row = block_number * block_rows
        query_block, bent_scores, allowed = block_scores(first_row, query_all, key_copies)
        exp_scores = jnp.where(allowed[None], jnp.exp(SOFT_CAP * bent_scores), 0.0)
        row_total = jnp.sum(exp_scores, axis=-1, keepdims=True)
        prob_rows = (exp_scores / row_total).astype(BF)
        head_outs.append(
            jnp.einsum("hqk,khd->qhd", prob_rows, value_copies, preferred_element_type=F32)
        )
        log_totals.append(jnp.log(row_total))
    attended = jnp.concatenate(head_outs, axis=0).astype(BF).reshape(group_size, q_cols)
    attn_mixed = scatter_t(dot_nt(attended, out_weight_t))
    scale_mix = inv_root(attn_mixed)
    middle = stream + attn_mixed * scale_mix * norm_scale[1]
    scale_mid = inv_root(middle)
    normed_ffn = (middle * scale_mid * norm_scale[2]).astype(BF)

    def ring(unit, work):
        units, chunks, partials = unit, [], []
        for k in range(nz):
            chunk = jnp.concatenate([units, grid.swap_y(units)], axis=0)
            if k + 1 < nz:
                units = grid.rot_z(units)
            chunks.append(chunk)
            partial = work(k, chunk)
            partials.append(
                partial[:rows] + grid.swap_y(partial[rows:].astype(BF)).astype(F32)
            )
        total = partials[1 % nz]
        for k in range(2, nz + 1):
            total = grid.rot_z(total.astype(BF)).astype(F32) + partials[k % nz]
        return total, chunks

    gates, ups, hiddens = [], [], []

    def forward_work(k, chunk):
        gate_out = dot_nn(chunk, gate_weight)
        up_out = dot_nn(chunk, up_weight)
        hidden = gated_unit(gate_out, up_out).astype(BF)
        gates.append(gate_out)
        ups.append(up_out)
        hiddens.append(hidden)
        return dot_nt(hidden, down_weight_t)

    branch, ffn_chunks = ring(normed_ffn, forward_work)
    scale_ffn = inv_root(branch)
    result = middle + branch * scale_ffn * norm_scale[3]
    upstream = cotangent.astype(F32)
    grad_branch, gain_last = norm_back(branch, scale_ffn, norm_scale[3], upstream)

    grad_gates, grad_ups = [], []

    def backward_work(k, chunk):
        grad_hidden = dot_nn(chunk, down_weight_t)
        unused_value, pullback = jax.vjp(gated_unit, gates[k], ups[k])
        grad_gate_out, grad_up_out = pullback(grad_hidden)
        grad_gate_out = grad_gate_out.astype(BF)
        grad_up_out = grad_up_out.astype(BF)
        grad_gates.append(grad_gate_out)
        grad_ups.append(grad_up_out)
        return dot_nt(grad_gate_out, gate_weight) + dot_nt(grad_up_out, up_weight)

    grad_normed_ffn, branch_chunks = ring(grad_branch.astype(BF), backward_work)

    ffn_all = jnp.concatenate(ffn_chunks, axis=0)
    grad_down_t = dot_tn(
        jnp.concatenate(branch_chunks, axis=0), jnp.concatenate(hiddens, axis=0)
    ).astype(BF)
    grad_w_gate = dot_tn(ffn_all, jnp.concatenate(grad_gates, axis=0)).astype(BF)
    grad_w_up = dot_tn(ffn_all, jnp.concatenate(grad_ups, axis=0)).astype(BF)

    def core_sum(grads):
        stack = grads.reshape(nz, 2, dpart, grads.shape[1])
        other = grid.swap_c(pick(stack, 1 - c, 1))
        return pick(stack, c, 1).astype(F32) + other.astype(F32)

    def collect(grads):
        total = core_sum(grads)
        kept = total[:, :, :slot]
        for j in range(1, nx):
            sent = total[:, :, j * slot : (j + 1) * slot].astype(BF)
            kept = kept + grid.xor_x(sent, j).astype(F32)
        kept = kept.astype(BF)
        buffer = jnp.zeros((nz, dpart, slot), BF)
        for k in range(nz):
            piece = pick(kept, (z + k) % nz)
            buffer = put(buffer, piece if k == 0 else grid.rot_z(piece, k), from_z[k])
        return buffer

    def rows_of(buffer):
        return jnp.transpose(buffer, (1, 0, 2)).reshape(dpart, hidden_part).astype(F32)

    down_buffer = collect(grad_down_t)
    grad_down = jnp.transpose(down_buffer, (0, 2, 1)).reshape(hidden_part, dpart).astype(F32)
    grad_gate = rows_of(collect(grad_w_gate))
    grad_up = rows_of(collect(grad_w_up))

    grad_mid_norm, gain_third = norm_back(middle, scale_mid, norm_scale[2], grad_normed_ffn)
    grad_middle = upstream + grad_mid_norm
    grad_mixed, gain_second = norm_back(attn_mixed, scale_mix, norm_scale[1], grad_middle)
    mixed_grads = gather_t(grad_mixed.astype(BF))
    grad_out_t = dot_tn(mixed_grads, attended).astype(BF)
    grad_attended = (
        dot_nn(mixed_grads, out_weight_t).astype(BF).reshape(group_size, local_heads, HD)
    )
    query_parts = []
    key_accum = jnp.zeros((group_size, local_heads, HD), F32)
    value_accum = jnp.zeros((group_size, local_heads, HD), F32)
    for block_number in range(block_count):
        first_row = block_number * block_rows
        query_block, bent_scores, allowed = block_scores(first_row, query_all, key_copies)
        prob_full = jnp.where(
            allowed[None], jnp.exp(SOFT_CAP * bent_scores - log_totals[block_number]), 0.0
        )
        grad_block = grad_attended[first_row : first_row + block_rows]
        grad_probs = jnp.einsum(
            "qhd,khd->hqk", grad_block, value_copies, preferred_element_type=F32
        )
        inner_sum = jnp.sum(prob_full * grad_probs, axis=-1, keepdims=True)
        grad_raw = (
            prob_full * (grad_probs - inner_sum) * (1.0 - bent_scores * bent_scores) * qk_scale
        ).astype(BF)
        query_parts.append(
            jnp.einsum("hqk,khd->qhd", grad_raw, key_copies, preferred_element_type=F32)
        )
        key_accum = key_accum + jnp.einsum(
            "hqk,qhd->khd", grad_raw, query_block, preferred_element_type=F32
        )
        value_accum = value_accum + jnp.einsum(
            "hqk,qhd->khd", prob_full.astype(BF), grad_block, preferred_element_type=F32
        )
    query_grads = jnp.concatenate(query_parts, axis=0).astype(BF).reshape(group_size, q_cols)
    key_grads = key_accum.astype(BF).reshape(group_size, q_cols)
    value_grads = value_accum.astype(BF).reshape(group_size, q_cols)

    def fold(columns):
        return columns.reshape(width, local_kv, copies, HD).sum(axis=2).reshape(width, kv_cols)

    key_columns = fold(dot_tn(attn_gathered, key_grads)).astype(BF)
    value_columns = fold(dot_tn(attn_gathered, value_grads)).astype(BF)
    grad_w_query = dot_tn(attn_gathered, query_grads).astype(BF)

    def widen(weight):
        return jnp.repeat(weight.reshape(width, local_kv, HD), copies, axis=1).reshape(
            width, q_cols
        )

    grads_joined = jnp.concatenate([query_grads, key_grads, value_grads], axis=1)
    weights_joined = jnp.concatenate(
        [
            qkv_weight[:, :q_cols],
            widen(qkv_weight[:, q_cols : q_cols + kv_cols]),
            widen(qkv_weight[:, q_cols + kv_cols :]),
        ],
        axis=1,
    )
    grad_normed_attn = scatter_t(dot_nt(grads_joined, weights_joined))
    grad_in_norm, gain_first = norm_back(stream, scale_in, norm_scale[0], grad_normed_attn)
    grad_tokens = grad_middle + grad_in_norm

    def ring_sum(grads):
        stack = core_sum(grads)
        total = pick(stack, from_z[1 % nz])
        for k in range(2, nz + 1):
            total = grid.rot_z(total.astype(BF)).astype(F32) + pick(stack, from_z[k % nz])
        return total

    grad_out = ring_sum(grad_out_t).T
    kv_sum = ring_sum(jnp.concatenate([key_columns, value_columns], axis=1)).astype(BF)
    grad_query = ring_sum(grad_w_query)

    kv_buffer = jnp.zeros((tp,) + kv_sum.shape, BF)
    for k in range(tp):
        kv_buffer = put(kv_buffer, kv_sum if k == 0 else grid.xor_t(kv_sum, k), t_index ^ k)
    sharers = tp * local_kv // KVH
    kv_full = kv_buffer.astype(F32).reshape(tp // sharers, sharers, dpart, 2, kv_cols).sum(axis=1)
    kv_full = jnp.transpose(kv_full, (2, 1, 0, 3)).reshape(2, dpart, KVH * HD)

    gain_stack = jnp.stack([gain_first, gain_second, gain_third, gain_last], axis=0)
    gain_parts = jnp.transpose(gain_stack.reshape(4, grid.dp, dpart), (1, 0, 2))
    gain_sum = pick(gain_parts, dp_index)
    for k in range(1, grid.dp):
        gain_sum = gain_sum + grid.xor_dp(pick(gain_parts, dp_index ^ k), k)
    gain_table = jnp.zeros((tp,) + gain_sum.shape, F32)
    for k in range(tp):
        gain_table = put(gain_table, gain_sum if k == 0 else grid.xor_t(gain_sum, k), t_index ^ k)
    grad_gains = gain_table.sum(axis=0)

    return (
        result,
        grad_tokens,
        grad_query,
        kv_full[0],
        kv_full[1],
        grad_out,
        grad_gate,
        grad_up,
        grad_down,
        grad_gains,
    )


def solution(mesh):
    grid = Grid(mesh.shape["dp"], mesh.shape["tensor"])

    def shards(*args):
        return program(grid, *args)

    in_specs = (
        P(("dp", "tensor"), None),
        P(("dp", "tensor"), None),
        P("dp", None),
        P("dp", "tensor"),
        P("dp", None),
        P("dp", None),
        P("tensor", "dp"),
        P("dp", "tensor"),
        P("dp", "tensor"),
        P("tensor", "dp"),
        P(None, "dp"),
    )
    out_specs = (
        P(("dp", "tensor"), None),
        P(("dp", "tensor"), None),
        P("dp", "tensor"),
        P("dp", None),
        P("dp", None),
        P("tensor", "dp"),
        P("dp", "tensor"),
        P("dp", "tensor"),
        P("tensor", "dp"),
        P(None, "dp"),
    )
    return jax.shard_map(shards, mesh=mesh, in_specs=in_specs, out_specs=out_specs, check_vma=False)
```

```python
import jax
import jax.numpy as jnp
from jax import lax
from jax.sharding import PartitionSpec as P

HQ = 8
KVH = 4
HD = 256

EPSILON = 1e-06
SOFT_CAP = 50.0
BF = jnp.bfloat16
F32 = jnp.float32
BOTH = ("dp", "tensor")


def inv_root(source):
    return lax.rsqrt(jnp.mean(source * source, axis=-1, keepdims=True) + EPSILON)


def norm_back(source, inverse, gain_row, upstream):
    unit_rows = source * inverse
    scaled = upstream * gain_row
    grad_input = inverse * (
        scaled - unit_rows * jnp.mean(scaled * unit_rows, axis=-1, keepdims=True)
    )
    return (grad_input, jnp.sum(upstream * unit_rows, axis=0))


def gated_unit(gate_in, up_in):
    return jax.nn.gelu(gate_in, approximate=True) * up_in


def dot_nn(left, right):
    return jnp.dot(left, right, preferred_element_type=F32)


def dot_nt(left, right):
    return lax.dot_general(left, right, (((1,), (1,)), ((), ())), preferred_element_type=F32)


def dot_tn(left, right):
    return lax.dot_general(left, right, (((0,), (0,)), ((), ())), preferred_element_type=F32)


class Grid:
    def __init__(self, dp, tp):
        self.dp, self.tp = dp, tp
        self.nz, self.nc = dp // 2, 2
        self.ny, self.nx = 2, tp // 2

    def coords(self, flat):
        d, t = divmod(flat, self.tp)
        z, c = divmod(d, self.nc)
        y, x = divmod(t, self.nx)
        return z, c, y, x

    def flat(self, z, c, y, x):
        return (z * self.nc + c) * self.tp + y * self.nx + x

    def move(self, value, where):
        pairs = []
        for i in range(self.dp * self.tp):
            pairs.append((i, self.flat(*where(*self.coords(i)))))
        return lax.ppermute(value, BOTH, pairs)

    def rot_z(self, value, k=1):
        return self.move(value, lambda z, c, y, x: ((z + k) % self.nz, c, y, x))

    def swap_c(self, value):
        return self.move(value, lambda z, c, y, x: (z, 1 - c, y, x))

    def swap_y(self, value):
        return self.move(value, lambda z, c, y, x: (z, c, 1 - y, x))

    def xor_x(self, value, k):
        return self.move(value, lambda z, c, y, x: (z, c, y, x ^ k))

    def xor_t(self, value, k):
        def where(z, c, y, x):
            t = (y * self.nx + x) ^ k
            return z, c, t // self.nx, t % self.nx

        return self.move(value, where)

    def xor_dp(self, value, k):
        def where(z, c, y, x):
            d = (z * self.nc + c) ^ k
            return d // self.nc, d % self.nc, y, x

        return self.move(value, where)


def pick(stack, index, axis=0):
    return lax.dynamic_index_in_dim(stack, index, axis, keepdims=False)


def put(buffer, piece, *indices):
    start = tuple(indices) + (0,) * (buffer.ndim - len(indices))
    shaped = piece.reshape((1,) * len(indices) + piece.shape)
    return lax.dynamic_update_slice(buffer, shaped, start)


def after(value, *needed):
    return lax.optimization_barrier((value, *needed))[0]


def program(
    grid,
    tokens,
    cotangent,
    doc_lengths,
    w_query,
    w_key,
    w_value,
    w_out,
    w_gate,
    w_up,
    w_down,
    norm_gains,
):
    nz, tp, nx = grid.nz, grid.tp, grid.nx
    dp_index = lax.axis_index("dp")
    t_index = lax.axis_index("tensor")
    z, c = dp_index // grid.nc, dp_index % grid.nc
    rows, width = tokens.shape
    dpart = w_query.shape[0]
    hidden_part = w_gate.shape[1]
    slot = hidden_part // nz
    group_size = rows * tp
    local_heads = w_query.shape[1] // HD
    local_kv = max(1, local_heads * KVH // HQ)
    copies = local_heads // local_kv
    kv_first = t_index * (local_heads * KVH) // HQ
    q_cols, kv_cols = local_heads * HD, local_kv * HD
    from_z = [(z - k) % nz for k in range(nz)]

    gains_other = grid.swap_c(norm_gains)
    gain_pair = jnp.where(
        c == 0, jnp.stack([norm_gains, gains_other]), jnp.stack([gains_other, norm_gains])
    )
    gain_buffer = jnp.zeros((nz,) + gain_pair.shape, BF)
    for k in range(nz):
        gain_buffer = put(gain_buffer, gain_pair if k == 0 else grid.rot_z(gain_pair, k), from_z[k])
    norm_scale = jnp.transpose(gain_buffer, (2, 0, 1, 3)).reshape(4, width).astype(F32)

    key_part = lax.dynamic_slice_in_dim(w_key, kv_first * HD, kv_cols, 1)
    value_part = lax.dynamic_slice_in_dim(w_value, kv_first * HD, kv_cols, 1)

    def gather_dp(local):
        pieces = [local]
        for k in range(1, nz):
            pieces.append(grid.rot_z(pieces[-1]))
        buffer = jnp.zeros((nz, 2) + local.shape, BF)
        for k in range(nz):
            buffer = put(buffer, pieces[k], from_z[k], c)
            buffer = put(buffer, grid.swap_c(pieces[k]), from_z[k], 1 - c)
        return buffer.reshape(width, local.shape[1]), pieces

    qkv_weight, qkv_pieces = gather_dp(jnp.concatenate([w_query, key_part, value_part], axis=1))
    out_weight_t, out_pieces = gather_dp(after(w_out.T, qkv_pieces[-1]))

    w_down_t = w_down.T
    slots = jnp.stack(
        [
            jnp.concatenate([m[:, i * slot : (i + 1) * slot] for m in (w_gate, w_up, w_down_t)], 1)
            for i in range(nz)
        ]
    )
    part = nx * slot
    slots = after(slots, out_pieces[-2])
    ffn_buffer = jnp.zeros((nz, 2, dpart, 3 * part), BF)
    for k in range(nz):
        mine = pick(slots, (z + k) % nz)
        piece = mine if k == 0 else grid.rot_z(mine, k)
        pieces = [piece] + [grid.xor_x(piece, j) for j in range(1, nx)]
        joined = jnp.concatenate(
            [p[:, m * slot : (m + 1) * slot] for m in range(3) for p in pieces], axis=1
        )
        ffn_buffer = put(ffn_buffer, joined, from_z[k], c)
        ffn_buffer = put(ffn_buffer, grid.swap_c(joined), from_z[k], 1 - c)
    ffn_buffer = ffn_buffer.reshape(width, 3 * part)
    pair_weight = ffn_buffer[:, : 2 * part]
    down_weight_t = ffn_buffer[:, 2 * part :]

    place_parts = [(t_index ^ k) * rows + jnp.arange(rows, dtype=jnp.int32) for k in range(tp)]
    places = jnp.concatenate(place_parts)
    doc_ends = jnp.cumsum(doc_lengths[0])
    inside = jnp.sum((doc_ends[None, :] <= places[:, None]).astype(jnp.int32), axis=1)
    segment = jnp.where(places >= doc_ends[-1], doc_lengths.shape[1] + places, inside)
    block_count = max(1, group_size // 512)
    block_rows = group_size // block_count
    qk_scale = HD ** (-0.5)

    def gather_t(unit):
        return jnp.concatenate([unit] + [grid.xor_t(unit, k) for k in range(1, tp)], axis=0)

    def scatter_t(partial):
        total = partial[:rows]
        for k in range(1, tp):
            total = total + grid.xor_t(partial[k * rows : (k + 1) * rows].astype(BF), k).astype(F32)
        return total

    def block_scores(first_row, query_all, key_copies):
        query_block = query_all[first_row : first_row + block_rows]
        raw_scores = jnp.einsum(
            "qhd,khd->hqk", query_block, key_copies, preferred_element_type=F32
        )
        bent_scores = jnp.tanh(raw_scores * (qk_scale / SOFT_CAP))
        row_segment = segment[first_row : first_row + block_rows]
        row_places = places[first_row : first_row + block_rows]
        allowed = (row_segment[:, None] == segment[None, :]) & (
            places[None, :] <= row_places[:, None]
        )
        return (query_block, bent_scores, allowed)

    stream = tokens.astype(F32)
    scale_in = inv_root(stream)
    normed_attn = (stream * scale_in * norm_scale[0]).astype(BF)
    attn_gathered = gather_t(normed_attn)
    qkv = dot_nn(attn_gathered, qkv_weight).astype(BF)
    query_all = qkv[:, :q_cols].reshape(group_size, local_heads, HD)
    key_heads = qkv[:, q_cols : q_cols + kv_cols].reshape(group_size, local_kv, HD)
    value_heads = qkv[:, q_cols + kv_cols :].reshape(group_size, local_kv, HD)
    key_copies = jnp.repeat(key_heads, copies, axis=1)
    value_copies = jnp.repeat(value_heads, copies, axis=1)
    head_outs = []
    log_totals = []
    for block_number in range(block_count):
        first_row = block_number * block_rows
        query_block, bent_scores, allowed = block_scores(first_row, query_all, key_copies)
        exp_scores = jnp.where(allowed[None], jnp.exp(SOFT_CAP * bent_scores), 0.0)
        row_total = jnp.sum(exp_scores, axis=-1, keepdims=True)
        prob_rows = (exp_scores / row_total).astype(BF)
        head_outs.append(
            jnp.einsum("hqk,khd->qhd", prob_rows, value_copies, preferred_element_type=F32)
        )
        log_totals.append(jnp.log(row_total))
    attended = jnp.concatenate(head_outs, axis=0).astype(BF).reshape(group_size, q_cols)
    attn_mixed = scatter_t(dot_nt(attended, out_weight_t))
    scale_mix = inv_root(attn_mixed)
    middle = stream + attn_mixed * scale_mix * norm_scale[1]
    scale_mid = inv_root(middle)
    normed_ffn = (middle * scale_mid * norm_scale[2]).astype(BF)

    def ring(unit, work):
        units, chunks, partials = unit, [], []
        for k in range(nz):
            chunk = jnp.concatenate([units, grid.swap_y(units)], axis=0)
            if k + 1 < nz:
                units = grid.rot_z(units)
            chunks.append(chunk)
            partial = work(k, chunk)
            partials.append(
                partial[:rows] + grid.swap_y(partial[rows:].astype(BF)).astype(F32)
            )
        total = partials[1 % nz]
        for k in range(2, nz + 1):
            total = grid.rot_z(total.astype(BF)).astype(F32) + partials[k % nz]
        return total, chunks

    pairs, hiddens = [], []

    def forward_work(k, chunk):
        pair = dot_nn(chunk, pair_weight)
        hidden = gated_unit(pair[:, :part], pair[:, part:]).astype(BF)
        pairs.append(pair)
        hiddens.append(hidden)
        return dot_nt(hidden, down_weight_t)

    branch, ffn_chunks = ring(normed_ffn, forward_work)
    scale_ffn = inv_root(branch)
    result = middle + branch * scale_ffn * norm_scale[3]
    upstream = cotangent.astype(F32)
    grad_branch, gain_last = norm_back(branch, scale_ffn, norm_scale[3], upstream)

    grad_pairs = []

    def backward_work(k, chunk):
        grad_hidden = dot_nn(chunk, down_weight_t)
        unused_value, pullback = jax.vjp(gated_unit, pairs[k][:, :part], pairs[k][:, part:])
        grad_gate_out, grad_up_out = pullback(grad_hidden)
        grad_pair = jnp.concatenate([grad_gate_out.astype(BF), grad_up_out.astype(BF)], axis=1)
        grad_pairs.append(grad_pair)
        return dot_nt(grad_pair, pair_weight)

    grad_normed_ffn, branch_chunks = ring(grad_branch.astype(BF), backward_work)

    grad_down_t = dot_tn(
        jnp.concatenate(branch_chunks, axis=0), jnp.concatenate(hiddens, axis=0)
    ).astype(BF)
    grad_pair_weight = dot_tn(
        jnp.concatenate(ffn_chunks, axis=0), jnp.concatenate(grad_pairs, axis=0)
    ).astype(BF)

    def core_sum(grads):
        stack = grads.reshape(nz, 2, dpart, grads.shape[1])
        other = grid.swap_c(pick(stack, 1 - c, 1))
        return pick(stack, c, 1).astype(F32) + other.astype(F32)

    def x_split(grads, mats):
        total = core_sum(grads)
        blocks = []
        for j in range(nx):
            columns = [
                total[:, :, (m * nx + j) * slot : (m * nx + j + 1) * slot] for m in range(mats)
            ]
            block = jnp.concatenate(columns, axis=2)
            blocks.append(block if j == 0 else block.astype(BF))
        return blocks

    def x_sum(blocks):
        total = blocks[0]
        for j in range(1, nx):
            total = total + grid.xor_x(blocks[j], j).astype(F32)
        return total.astype(BF)

    def z_exchange(stack):
        return [
            pick(stack, (z + k) % nz) if k == 0 else grid.rot_z(pick(stack, (z + k) % nz), k)
            for k in range(nz)
        ]

    def in_order(pieces, m):
        pieces = [p[:, m * slot : (m + 1) * slot] for p in pieces]
        blocks = []
        for b in range(nz):
            block = pieces[(-b) % nz]
            for i in range(1, nz):
                block = jnp.where(z == i, pieces[(i - b) % nz], block)
            blocks.append(block)
        return jnp.concatenate(blocks, axis=1).astype(F32)

    down_blocks = x_split(grad_down_t, 1)
    pair_blocks = x_split(grad_pair_weight, 2)

    grad_mid_norm, gain_third = norm_back(middle, scale_mid, norm_scale[2], grad_normed_ffn)
    grad_middle = upstream + grad_mid_norm
    grad_mixed, gain_second = norm_back(attn_mixed, scale_mix, norm_scale[1], grad_middle)
    mixed_grads = gather_t(grad_mixed.astype(BF))
    mixed_grads = after(mixed_grads, down_blocks[1], pair_blocks[1])
    grad_out_t = dot_tn(mixed_grads, attended).astype(BF)
    grad_attended = (
        dot_nn(mixed_grads, out_weight_t).astype(BF).reshape(group_size, local_heads, HD)
    )
    down_sum = x_sum(down_blocks)
    pair_sum = x_sum(pair_blocks)
    grad_attended = after(grad_attended, down_sum, pair_sum)
    down_pieces = z_exchange(down_sum)
    pair_pieces = z_exchange(pair_sum)
    query_parts = []
    key_accum = jnp.zeros((group_size, local_heads, HD), F32)
    value_accum = jnp.zeros((group_size, local_heads, HD), F32)
    for block_number in range(block_count):
        first_row = block_number * block_rows
        query_block, bent_scores, allowed = block_scores(first_row, query_all, key_copies)
        prob_full = jnp.where(
            allowed[None], jnp.exp(SOFT_CAP * bent_scores - log_totals[block_number]), 0.0
        )
        grad_block = grad_attended[first_row : first_row + block_rows]
        grad_probs = jnp.einsum(
            "qhd,khd->hqk", grad_block, value_copies, preferred_element_type=F32
        )
        inner_sum = jnp.sum(prob_full * grad_probs, axis=-1, keepdims=True)
        grad_raw = (
            prob_full * (grad_probs - inner_sum) * (1.0 - bent_scores * bent_scores) * qk_scale
        ).astype(BF)
        query_parts.append(
            jnp.einsum("hqk,khd->qhd", grad_raw, key_copies, preferred_element_type=F32)
        )
        key_accum = key_accum + jnp.einsum(
            "hqk,qhd->khd", grad_raw, query_block, preferred_element_type=F32
        )
        value_accum = value_accum + jnp.einsum(
            "hqk,qhd->khd", prob_full.astype(BF), grad_block, preferred_element_type=F32
        )
    query_grads = jnp.concatenate(query_parts, axis=0).astype(BF).reshape(group_size, q_cols)
    key_grads = key_accum.astype(BF).reshape(group_size, q_cols)
    value_grads = value_accum.astype(BF).reshape(group_size, q_cols)

    def fold(columns):
        return columns.reshape(width, local_kv, copies, HD).sum(axis=2).reshape(width, kv_cols)

    key_columns = fold(dot_tn(attn_gathered, key_grads)).astype(BF)
    value_columns = fold(dot_tn(attn_gathered, value_grads)).astype(BF)
    grad_w_query = dot_tn(attn_gathered, query_grads).astype(BF)

    def widen(weight):
        return jnp.repeat(weight.reshape(width, local_kv, HD), copies, axis=1).reshape(
            width, q_cols
        )

    grads_joined = jnp.concatenate([query_grads, key_grads, value_grads], axis=1)
    weights_joined = jnp.concatenate(
        [
            qkv_weight[:, :q_cols],
            widen(qkv_weight[:, q_cols : q_cols + kv_cols]),
            widen(qkv_weight[:, q_cols + kv_cols :]),
        ],
        axis=1,
    )
    grad_normed_attn = scatter_t(dot_nt(grads_joined, weights_joined))
    grad_in_norm, gain_first = norm_back(stream, scale_in, norm_scale[0], grad_normed_attn)
    grad_tokens = grad_middle + grad_in_norm

    def ring_sum(grads):
        stack = core_sum(grads)
        total = pick(stack, from_z[1 % nz])
        for k in range(2, nz + 1):
            total = grid.rot_z(total.astype(BF)).astype(F32) + pick(stack, from_z[k % nz])
        return total

    grad_out = ring_sum(grad_out_t).T
    kv_sum = ring_sum(jnp.concatenate([key_columns, value_columns], axis=1)).astype(BF)
    grad_query = ring_sum(grad_w_query)

    kv_buffer = jnp.zeros((tp,) + kv_sum.shape, BF)
    for k in range(tp):
        kv_buffer = put(kv_buffer, kv_sum if k == 0 else grid.xor_t(kv_sum, k), t_index ^ k)
    sharers = tp * local_kv // KVH
    kv_full = kv_buffer.astype(F32).reshape(tp // sharers, sharers, dpart, 2, kv_cols).sum(axis=1)
    kv_full = jnp.transpose(kv_full, (2, 1, 0, 3)).reshape(2, dpart, KVH * HD)

    gain_stack = jnp.stack([gain_first, gain_second, gain_third, gain_last], axis=0)
    gain_parts = jnp.transpose(gain_stack.reshape(4, grid.dp, dpart), (1, 0, 2))
    gain_sum = pick(gain_parts, dp_index)
    for k in range(1, grid.dp):
        gain_sum = gain_sum + grid.xor_dp(pick(gain_parts, dp_index ^ k), k)
    gain_table = jnp.zeros((tp,) + gain_sum.shape, F32)
    for k in range(tp):
        gain_table = put(gain_table, gain_sum if k == 0 else grid.xor_t(gain_sum, k), t_index ^ k)
    grad_gains = gain_table.sum(axis=0)

    grad_gate = in_order(pair_pieces, 0)
    grad_up = in_order(pair_pieces, 1)
    grad_down = in_order(down_pieces, 0).T

    return (
        result,
        grad_tokens,
        grad_query,
        kv_full[0],
        kv_full[1],
        grad_out,
        grad_gate,
        grad_up,
        grad_down,
        grad_gains,
    )


def solution(mesh):
    grid = Grid(mesh.shape["dp"], mesh.shape["tensor"])

    def shards(*args):
        return program(grid, *args)

    in_specs = (
        P(("dp", "tensor"), None),
        P(("dp", "tensor"), None),
        P("dp", None),
        P("dp", "tensor"),
        P("dp", None),
        P("dp", None),
        P("tensor", "dp"),
        P("dp", "tensor"),
        P("dp", "tensor"),
        P("tensor", "dp"),
        P(None, "dp"),
    )
    out_specs = (
        P(("dp", "tensor"), None),
        P(("dp", "tensor"), None),
        P("dp", "tensor"),
        P("dp", None),
        P("dp", None),
        P("tensor", "dp"),
        P("dp", "tensor"),
        P("dp", "tensor"),
        P("tensor", "dp"),
        P(None, "dp"),
    )
    return jax.shard_map(shards, mesh=mesh, in_specs=in_specs, out_specs=out_specs, check_vma=False)
```
